32 devices in a mesh: grp: 4 (over y, x), body: 8 (over z, core).
Axes of the slice: x: 2, y: 2, z: 4, core: 2. Of those that a mesh axis runs over, the one named last changes fastest.
Arguments:
- incident: bfloat16 [32, 16, 512], P(('grp', 'body')), may hold values from -6 to 6
- exciting: float32 [32, 16, 512], P(('grp', 'body')), may hold values from -6 to 6
- t_matrices: bfloat16 [32, 2, 256, 256], P(('grp', 'body')), may hold values from -0.1875 to 0.1875
- hankel_rows: bfloat16 [225, 2, 512], replicated, may hold values from -0.09375 to 0.09375
- offsets: int32 [32, 8], P(('grp', 'body')), may hold values from 0 to 224
- lattice_slots: int32 [32], P('grp'), may hold values from 0 to 7, as said below
- up_maps: bfloat16 [32, 2, 256, 512], P(('grp', 'body')), may hold values from -0.125 to 0.125
- down_maps: bfloat16 [32, 2, 512, 256], P(('grp', 'body')), may hold values from -0.1875 to 0.1875
- group_maps: bfloat16 [4, 4, 2, 512, 512], P('grp', None, None, 'body'), may hold values from -0.09375 to 0.09375
Outputs:
- updated: float32 [32, 16, 512], P(('grp', 'body'))
The draws below stay inside these ranges and needn't reach their ends.
Inputs may be any that keep to these rules, and one draw needn't show every extreme that they name: `lattice_slots`: within each group the 8 columns stand at the slots 0 to 7, one column a slot.
All inputs are finite; a program needn't handle non-finite values.
Results may differ from the reference program's by a relative error of at most 0.0034.
Values may be sent and summed in bfloat16 or wider, within the bound.
No kernel may reach another device: no remote copies, remote signals or barrier semaphores. Data moves between devices by JAX's collectives and lax.ppermute only.
A program may use at most 64 MiB of HBM per device.

```python
import jax
import jax.numpy as jnp
from jax import lax

P_SIZE = 256
Q = 512
L = 16
NTAB = 225
G = 4
GB = 8
NB = 32


def draw_lattice_slots(key, part):
    group_keys = jax.random.split(jax.random.fold_in(key, 11), G)
    orders = jax.vmap(lambda group_key: jax.random.permutation(group_key, GB))(group_keys)
    return orders.reshape(-1).astype(jnp.int32)


def set_ends(values, key, smallest, high):
    extent = values.shape
    spot = [jax.random.randint(jax.random.fold_in(key, axis), (), 0, extent[axis]) for axis in range(len(extent))]
    values = values.at[tuple(spot)].set(smallest)
    longest = extent.index(max(extent))
    spot[longest] = (spot[longest] + 1) % extent[longest]
    return values.at[tuple(spot)].set(high)


def block_scale(own_key, dims, pieces, smallest, largest):
    loudness = 1.0
    for dim, parts in pieces:
        heights = jax.random.uniform(jax.random.fold_in(jax.random.fold_in(own_key, 6), dim), (parts,), jnp.float32, smallest / len(pieces), largest / len(pieces))
        loudness = loudness * jnp.repeat(jnp.exp(heights), dims[dim] // parts).reshape((-1,) + (1,) * (len(dims) - 1 - dim))
    return loudness


def normal_values(key, shape, width, bound, shards=(), kind=jnp.bfloat16):
    drawn = jax.random.normal(key, shape, jnp.float32) * width
    if len(shards) > 0:
        drawn = block_scale(key, shape, shards, -0.22, 0.18) * drawn
    return jnp.clip(drawn, min=-bound, max=bound).astype(kind)


def setup_inputs(seed: int = 0) -> dict:
    splits = jax.random.split(jax.random.key(seed), 10)
    incident = normal_values(splits[0], (NB, L, 2 * P_SIZE), 1.0, 6.0, ((0, 32),))
    exciting = normal_values(splits[1], (NB, L, 2 * P_SIZE), 1.0, 6.0, ((0, 32),), jnp.float32)
    t_matrices = normal_values(splits[2], (NB, 2, P_SIZE, P_SIZE), (4 * P_SIZE) ** -0.5, 0.1875, ((0, 32),))
    hankel_rows = normal_values(splits[3], (NTAB, 2, 2 * P_SIZE), (2 * P_SIZE * GB) ** -0.5, 0.09375)
    offsets = set_ends(jax.random.randint(splits[4], (NB, GB), 0, NTAB), jax.random.fold_in(splits[4], 1), 0, NTAB - 1).astype(jnp.int32)
    lattice_slots = draw_lattice_slots(jax.random.fold_in(splits[9], 71), 0)
    up_maps = normal_values(splits[6], (NB, 2, P_SIZE, Q), (P_SIZE * GB) ** -0.5, 0.125, ((0, 32),))
    down_maps = normal_values(splits[7], (NB, 2, Q, P_SIZE), (2 * Q) ** -0.5, 0.1875, ((0, 32),))
    group_maps = normal_values(splits[8], (G, G, 2, Q, Q), (2 * Q * G) ** -0.5, 0.09375, ((0, 4), (3, 8)))
    return dict(incident=incident, exciting=exciting, t_matrices=t_matrices, hankel_rows=hankel_rows, offsets=offsets, lattice_slots=lattice_slots, up_maps=up_maps, down_maps=down_maps, group_maps=group_maps)


def complex_apply(form, values, real_mats, imag_mats):
    half_width = values.shape[-1] // 2
    real_values = values[..., :half_width].astype(jnp.float32)
    imag_values = values[..., half_width:].astype(jnp.float32)
    real_mats = real_mats.astype(jnp.float32)
    imag_mats = imag_mats.astype(jnp.float32)
    real_out = jnp.einsum(form, real_values, real_mats) - jnp.einsum(form, imag_values, imag_mats)
    imag_out = jnp.einsum(form, real_values, imag_mats) + jnp.einsum(form, imag_values, real_mats)
    return jnp.concatenate([real_out, imag_out], axis=-1)


def toeplitz_mats(sequences):
    length = sequences.shape[-1] // 2
    row_index = jnp.arange(length, dtype=jnp.int32)[:, None]
    col_index = jnp.arange(length, dtype=jnp.int32)[None, :]
    return sequences[..., length + col_index - row_index]


def reference(incident, exciting, t_matrices, hankel_rows, offsets, lattice_slots, up_maps, down_maps, group_maps):
    def scatter_one(inputs):
        values, mats = inputs
        return complex_apply("ln,nm->lm", values, mats[0], mats[1]).astype(jnp.bfloat16)

    scattered = lax.map(scatter_one, (incident, t_matrices))
    grouped = scattered.reshape(G, GB, L, 2 * P_SIZE)
    members = jnp.arange(GB, dtype=jnp.int32)
    zero_seq = jnp.zeros((), hankel_rows.dtype)

    def group_near(inputs):
        group_values, group_offsets, group_slots = inputs

        def target_near(target):
            offset_row, position = target
            sequences = hankel_rows[offset_row[group_slots]]
            sequences = jnp.where((members != position)[:, None, None], sequences, zero_seq)
            mats = toeplitz_mats(sequences)
            return complex_apply("jln,jnm->lm", group_values, mats[:, 0], mats[:, 1])

        return lax.map(target_near, (group_offsets, members))

    near = lax.map(group_near, (grouped, offsets.reshape(G, GB, GB), lattice_slots.reshape(G, GB)))
    near = near.reshape(NB, L, 2 * P_SIZE)

    def expand_one(inputs):
        values, mats = inputs
        return complex_apply("ln,nq->lq", values, mats[0], mats[1])

    terms = lax.map(expand_one, (scattered, up_maps))
    expansion = jnp.sum(terms.reshape(G, GB, L, 2 * Q), axis=1).astype(jnp.bfloat16)
    group_ids = jnp.arange(G, dtype=jnp.int32)

    def incoming_one(inputs):
        row_maps, destination = inputs

        def add_source(total, source):
            values, mats, source_id = source
            term = complex_apply("ln,nq->lq", values, mats[0], mats[1])
            return total + jnp.where(source_id == destination, jnp.float32(0.0), term), None

        total, _ = lax.scan(add_source, jnp.zeros((L, 2 * Q), jnp.float32), (expansion, row_maps, group_ids))
        return total

    incoming = lax.map(incoming_one, (group_maps, group_ids)).astype(jnp.bfloat16)

    def far_one(inputs):
        mats, column = inputs
        values = incoming[column // GB]
        return complex_apply("lq,qp->lp", values, mats[0], mats[1])

    far = lax.map(far_one, (down_maps, jnp.arange(NB, dtype=jnp.int32)))
    return exciting + near + far
```

```python
import functools

import jax
import jax.numpy as jnp
from jax import lax
from jax.experimental import pallas as pl
from jax.experimental.pallas import tpu as pltpu
from jax.sharding import PartitionSpec as P

AXES = ("grp", "body")
SMEM = pl.BlockSpec(memory_space=pltpu.SMEM)
VMEM = pl.BlockSpec(memory_space=pltpu.VMEM)


def crossed(values):
    rows = values.shape[0] // 2
    real, imag = values[:rows], values[rows:]
    return jnp.concatenate(
        [jnp.concatenate([real, -imag], axis=1), jnp.concatenate([imag, real], axis=1)], axis=0
    )


def dot(left, right):
    return jnp.dot(left, right, preferred_element_type=jnp.float32)


def first_kernel(core, incident, offsets, t_mats, up, scattered, partial_sum, message):
    rows, modes = incident.shape[0], t_mats.shape[2]
    values = jnp.concatenate([incident[:, :modes], incident[:, modes:]], axis=0)
    own = dot(crossed(values), t_mats[...].reshape(2 * modes, modes)).astype(jnp.bfloat16)
    scattered[...] = own
    term = dot(crossed(own), up[...].reshape(2 * modes, up.shape[2]))
    partial_sum[...] = term

    @pl.when(core[0] == 0)
    def _():
        message[...] = term

    @pl.when(core[0] != 0)
    def _():
        message[:, :modes] = own.astype(jnp.float32)
        message[:, modes:] = jnp.zeros((2 * rows, message.shape[1] - modes), jnp.float32)
        message[0:1, modes : modes + offsets.shape[1]] = offsets[...].astype(jnp.float32)


def near_kernel(where, offsets, slots, table, pieces, near):
    chips, _, rows, modes = pieces.shape
    half = modes // 2

    @pl.when(where[0] == 0)
    def _():
        chip = where[1]
        for column in range(2):
            total = jnp.zeros((rows, 2 * modes), jnp.float32)
            for other in range(chips):
                for member in range(2):
                    source = (chip ^ other) * 2 + member
                    row = offsets[column, slots[source]]
                    sequence = table[row].astype(jnp.float32)
                    if other == 0 and member == column:
                        continue
                    mats = []
                    for part in range(2):
                        band = jnp.broadcast_to(sequence[part : part + 1], (half, 2 * modes))
                        band = pltpu.roll(band, 0, 1, stride=1, stride_axis=0)
                        band = band.astype(jnp.bfloat16)
                        mats.append(
                            jnp.concatenate(
                                [band[:, modes:], band[:, half : half + modes]], axis=0
                            )
                        )
                    total += dot(pieces[other, member], jnp.concatenate(mats, axis=1))
            top, low = total[: rows // 2], total[rows // 2 :]
            near[column, : rows // 2, :] = top[:, :modes] - low[:, modes:]
            near[column, rows // 2 :, :] = top[:, modes:] + low[:, :modes]


def group_kernel(where, pieces, own_maps, other_maps, incoming):
    groups, rows, width = pieces.shape
    total = jnp.zeros(incoming.shape, jnp.float32)
    for other in range(1, groups):
        source = where[0] ^ other
        mats = jnp.concatenate(
            [other_maps[source, 0], own_maps[source, 0], other_maps[source, 1], own_maps[source, 1]],
            axis=0,
        )
        total += dot(crossed(pieces[other]), mats)
    incoming[...] = total


def last_kernel(incoming, near, down, exciting, updated):
    modes = down.shape[2]
    rows = exciting.shape[0]
    far = dot(crossed(incoming[...]), down[...].reshape(2 * down.shape[1], modes)) + near[...]
    updated[:, :modes] = exciting[:, :modes] + far[:rows]
    updated[:, modes:] = exciting[:, modes:] + far[rows:]


def digits(count):
    found, shift = [], 0
    while (1 << shift) < count:
        found.append([k << shift for k in range(1, min(4, count >> shift))])
        shift += 2
    return found


def local(
    groups,
    bodies,
    incident,
    exciting,
    t_matrices,
    hankel_rows,
    offsets,
    lattice_slots,
    up_maps,
    down_maps,
    group_maps,
):
    body = lax.axis_index("body")
    group = lax.axis_index("grp")
    core, chip = body % 2, body // 2
    chips = bodies // 2
    rows, modes = incident.shape[1], t_matrices.shape[2]
    coefs = up_maps.shape[3]
    bf16, f32 = jnp.bfloat16, jnp.float32

    def exchange(values, even, odd):
        pairs = [(i, i ^ (odd if i % 2 else even)) for i in range(groups * bodies)]
        return lax.ppermute(values, AXES, pairs)

    def shaped(shape, dtype):
        return jax.ShapeDtypeStruct(shape, dtype)

    core_arg = core.astype(jnp.int32).reshape(1)
    other_maps = exchange(group_maps[0], 1, 1)
    scattered, partial_sum, message = pl.pallas_call(
        first_kernel,
        out_shape=(
            shaped((2 * rows, modes), bf16),
            shaped((2 * rows, coefs), f32),
            shaped((2 * rows, coefs), f32),
        ),
        in_specs=[SMEM] + [VMEM] * 4,
        out_specs=(VMEM,) * 3,
        name="first",
    )(core_arg, incident[0], offsets, t_matrices[0], up_maps[0])
    received = exchange(message, 1, 1)

    expansion = partial_sum + received
    pieces = jnp.stack([scattered, received[:, :modes].astype(bf16)])[None]
    both_offsets = jnp.concatenate(
        [offsets, received[0:1, modes : modes + offsets.shape[1]].astype(jnp.int32)], axis=0
    )
    for steps in digits(chips):
        sums = jnp.stack([expansion[:, :modes], expansion[:, modes:]]).astype(bf16)[None]
        sums = jnp.pad(sums, ((0, pieces.shape[0] - 1), (0, 0), (0, 0), (0, 0)))
        message = jnp.where(core == 1, sums, pieces)
        arrived = [exchange(message, 2 * step, 2 * step) for step in steps]
        for piece in arrived:
            expansion += jnp.concatenate([piece[0, 0], piece[0, 1]], axis=1).astype(f32)
        pieces = jnp.concatenate([pieces] + arrived, axis=0)
    block = coefs // chips
    own_block = lax.dynamic_slice_in_dim(expansion, chip * block, block, 1).astype(bf16)[None]

    near = pl.pallas_call(
        near_kernel,
        out_shape=shaped((2, 2 * rows, modes), f32),
        in_specs=[SMEM] * 3 + [VMEM] * 2,
        out_specs=VMEM,
        name="near",
    )(jnp.stack([core, chip]).astype(jnp.int32), both_offsets, lattice_slots, hankel_rows, pieces)

    blocks = own_block
    for steps in digits(groups):
        arrived = [exchange(blocks, 2, step * bodies) for step in steps]
        blocks = jnp.concatenate([blocks] + arrived, axis=0)
    incoming = pl.pallas_call(
        group_kernel,
        out_shape=shaped((2 * rows, coefs), f32),
        in_specs=[SMEM] + [VMEM] * 3,
        out_specs=VMEM,
        name="group",
    )(group.astype(jnp.int32).reshape(1), blocks, group_maps[0], other_maps)
    for steps in digits(chips):
        message = incoming.astype(bf16)
        for piece in [exchange(message, bodies, 2 * step) for step in steps]:
            incoming += piece.astype(f32)

    message = jnp.where(
        core == 1, incoming, jnp.pad(near[1], ((0, 0), (0, coefs - modes)))
    )
    received = exchange(message, 1, 1)
    incoming = jnp.where(core == 1, incoming, received).astype(bf16)
    near = jnp.where(core == 1, received[:, :modes], near[0])
    return pl.pallas_call(
        last_kernel,
        out_shape=shaped((rows, 2 * modes), f32),
        in_specs=[VMEM] * 4,
        out_specs=VMEM,
        name="last",
    )(incoming, near, down_maps[0], exciting[0])[None]


def solution(mesh):
    return jax.shard_map(
        functools.partial(local, mesh.shape["grp"], mesh.shape["body"]),
        mesh=mesh,
        in_specs=(
            P(("grp", "body"), None, None),
            P(("grp", "body"), None, None),
            P(("grp", "body"), None, None, None),
            P(),
            P(("grp", "body"), None),
            P("grp"),
            P(("grp", "body"), None, None, None),
            P(("grp", "body"), None, None, None),
            P("grp", None, None, "body", None),
        ),
        out_specs=P(("grp", "body"), None, None),
        check_vma=False,
    )
```

```python
import functools

import jax
import jax.numpy as jnp
from jax import lax
from jax.experimental import pallas as pl
from jax.experimental.pallas import tpu as pltpu
from jax.sharding import PartitionSpec as P

AXES = ("grp", "body")
SMEM = pl.BlockSpec(memory_space=pltpu.SMEM)
VMEM = pl.BlockSpec(memory_space=pltpu.VMEM)
HBM = pl.BlockSpec(memory_space=pltpu.HBM)
PARAMS = pltpu.CompilerParams(vmem_limit_bytes=8 << 20)
BF16, F32 = jnp.bfloat16, jnp.float32


def crossed(values):
    rows = values.shape[0] // 2
    real, imag = values[:rows], values[rows:]
    return jnp.concatenate(
        [jnp.concatenate([real, -imag], axis=1), jnp.concatenate([imag, real], axis=1)], axis=0
    )


def dot(left, right):
    return jnp.dot(left, right, preferred_element_type=F32)


def shaped(shape, dtype):
    return jax.ShapeDtypeStruct(shape, dtype)


def in_hbm(*arrays):
    return [pltpu.with_memory_space_constraint(array, pltpu.HBM) for array in arrays]


def first_kernel(
    incident_hbm, offsets_hbm, t_hbm, up_hbm, scattered, message, incident, offsets, t_mats, up, sems
):
    sources = (incident_hbm, t_hbm, offsets_hbm, up_hbm)
    targets = (incident, t_mats, offsets, up)
    copies = [
        pltpu.make_async_copy(source, target, sems.at[i])
        for i, (source, target) in enumerate(zip(sources, targets))
    ]
    for copy in copies:
        copy.start()
    modes, coefs = up.shape[1:]
    rows = 2 * incident.shape[0]
    copies[0].wait()
    values = jnp.concatenate([incident[:, :modes], incident[:, modes:]], axis=0)
    values = crossed(values)
    copies[1].wait()
    own = dot(values, t_mats[...].reshape(2 * modes, modes)).astype(BF16)
    scattered[...] = own
    message[:rows, coefs:] = own.astype(F32)
    copies[2].wait()
    message[rows:, :] = jnp.zeros((message.shape[0] - rows, coefs + modes), F32)
    message[rows : rows + 1, : offsets.shape[1]] = offsets[...].astype(F32)
    own = crossed(own)
    copies[3].wait()
    message[:rows, :coefs] = dot(own, up[...].reshape(2 * modes, coefs))


def first_call(incident, offsets, t_mats, up):
    rows, modes, coefs = 2 * incident.shape[0], up.shape[1], up.shape[2]
    return pl.pallas_call(
        first_kernel,
        out_shape=(
            shaped((rows, modes), BF16),
            shaped((rows + 8, coefs + modes), F32),
        ),
        in_specs=[HBM] * 4,
        out_specs=(VMEM, VMEM),
        scratch_shapes=[
            pltpu.VMEM(incident.shape, BF16),
            pltpu.VMEM(offsets.shape, jnp.int32),
            pltpu.VMEM(t_mats.shape, BF16),
            pltpu.VMEM(up.shape, BF16),
            pltpu.SemaphoreType.DMA((4,)),
        ],
        compiler_params=PARAMS,
        name="first",
    )(*in_hbm(incident, offsets, t_mats, up))


def near_kernel(places, members, core, chip, indices, exciting_hbm, table, *rest):
    pieces, (near, exciting, sem) = rest[:-3], rest[-3:]
    copy = pltpu.make_async_copy(exciting_hbm, exciting, sem)
    copy.start()
    _, rows, modes = near.shape
    half = modes // 2

    @pl.when(core[0] == 1)
    def _():
        for column in range(2):
            total = jnp.zeros((rows, 2 * modes), F32)
            for other, piece, lane in places:
                for member in range(2):
                    if other == 0 and member == column:
                        continue
                    source = (chip[0] ^ other) * 2 + member
                    slot = indices[2 * members + source]
                    sequence = table[indices[column * members + slot]].astype(F32)
                    mats = []
                    for part in range(2):
                        band = jnp.broadcast_to(sequence[part : part + 1], (half, 2 * modes))
                        band = pltpu.roll(band, 0, 1, stride=1, stride_axis=0)
                        band = band.astype(BF16)
                        mats.append(
                            jnp.concatenate(
                                [band[:, modes:], band[:, half : half + modes]], axis=0
                            )
                        )
                    start = lane + member * modes
                    values = pieces[piece][:, start : start + modes]
                    total += dot(values, jnp.concatenate(mats, axis=1))
            top, low = total[: rows // 2], total[rows // 2 :]
            near[column, : rows // 2, :] = top[:, :modes] - low[:, modes:]
            near[column, rows // 2 :, :] = top[:, modes:] + low[:, :modes]

    copy.wait()


def group_kernel(places, group, own_maps, other_maps, *rest):
    pieces, incoming = rest[:-1], rest[-1]
    total = jnp.zeros(incoming.shape, F32)
    for other, piece, index in places:
        source = group[0] ^ other
        mats = jnp.concatenate(
            [other_maps[source, 0], own_maps[source, 0], other_maps[source, 1], own_maps[source, 1]],
            axis=0,
        )
        total += dot(crossed(pieces[piece][index]), mats)
    incoming[...] = total


def last_kernel(core, incoming, near, received, down, exciting, updated):
    coefs, modes = down.shape[1:]
    rows = exciting.shape[0]

    def finish(values, close):
        far = dot(crossed(values.astype(BF16)), down[...].reshape(2 * coefs, modes)) + close
        updated[:, :modes] = exciting[:, :modes] + far[:rows]
        updated[:, modes:] = exciting[:, modes:] + far[rows:]

    @pl.when(core[0] == 0)
    def _():
        finish(received[:, :coefs], received[:, coefs:])

    @pl.when(core[0] == 1)
    def _():
        finish(incoming[...], near[1])


def digits(count):
    bits = count.bit_length() - 1
    found = []
    while bits > 0:
        shift = bits - 2 if bits >= 2 else 0
        found.append([k << shift for k in range((1 << (bits - shift)) - 1, 0, -1)])
        bits = shift
    return found


def local(
    groups,
    bodies,
    incident,
    exciting,
    t_matrices,
    hankel_rows,
    offsets,
    lattice_slots,
    up_maps,
    down_maps,
    group_maps,
):
    body = lax.axis_index("body")
    group = lax.axis_index("grp")
    core, chip = body & 1, body >> 1
    chips = bodies // 2
    modes, coefs = up_maps.shape[2:]

    def exchange(values, even, odd):
        pairs = [(i, i ^ (odd if i % 2 else even)) for i in range(groups * bodies)]
        return lax.ppermute(values, AXES, pairs)

    core_at, chip_at, group_at = (x.astype(jnp.int32).reshape(1) for x in (core, chip, group))
    scattered, message = first_call(incident[0], offsets, t_matrices[0], up_maps[0])
    rows = scattered.shape[0]
    received = exchange(message, 1, 1)
    other_maps = exchange(group_maps[0], 1, 1)

    expansion = message[:rows, :coefs] + received[:rows, :coefs]
    members = offsets.shape[1]
    indices = jnp.concatenate(
        [received[rows, :members].astype(jnp.int32), offsets[0], lattice_slots], axis=0
    )
    pieces = [jnp.concatenate([received[:rows, coefs:].astype(BF16), scattered], axis=1)]
    places = [(0, 0, 0)]
    aside = bodies if groups > 1 else 2
    for steps in digits(chips):
        width = expansion.shape[1] // (len(steps) + 1)
        unit = min(steps)
        own = (chip // unit) % (len(steps) + 1)

        def part(index):
            return lax.dynamic_slice_in_dim(expansion, index * width, width, 1)

        gathered = [pieces[p][:, lane : lane + 2 * modes] for _, p, lane in places]
        messages = [
            jnp.concatenate(gathered + [part(own ^ (step // unit)).astype(BF16)], axis=1)
            for step in steps
        ]
        arrived = [exchange(m, aside, 2 * step) for m, step in zip(messages, steps)]
        held = len(places)
        expansion = part(own)
        for step, piece in zip(steps, arrived):
            expansion += piece[:, 2 * modes * held :].astype(F32)
            places += [
                (other ^ step, len(pieces), 2 * modes * i)
                for i, (other, _, _) in enumerate(places[:held])
            ]
            pieces.append(piece)

    near, exciting_near = pl.pallas_call(
        functools.partial(near_kernel, tuple(places), members),
        out_shape=(shaped((2, rows, modes), F32), shaped(exciting.shape[1:], F32)),
        in_specs=[SMEM] * 3 + [HBM, VMEM] + [VMEM] * len(pieces),
        out_specs=(VMEM, VMEM),
        scratch_shapes=[pltpu.SemaphoreType.DMA],
        compiler_params=PARAMS,
        name="near",
    )(core_at, chip_at, indices, *in_hbm(exciting[0]), hankel_rows, *pieces)

    blocks = [expansion.astype(BF16)[None]]
    group_places = [(0, 0, 0)]
    for steps in digits(groups):
        message = [blocks[b][i] for _, b, i in group_places]
        message = blocks[0] if len(message) == 1 else jnp.stack(message)
        held = list(group_places)
        for step in reversed(steps):
            group_places += [(other ^ step, len(blocks), i) for i, (other, _, _) in enumerate(held)]
            blocks.append(exchange(message, 2, step * bodies))
    incoming = pl.pallas_call(
        functools.partial(group_kernel, tuple(group_places[1:])),
        out_shape=shaped((rows, coefs), F32),
        in_specs=[SMEM] + [VMEM] * (2 + len(blocks)),
        out_specs=VMEM,
        compiler_params=PARAMS,
        name="group",
    )(group_at, group_maps[0], other_maps, *blocks)

    for steps in digits(chips):
        message = incoming.astype(BF16)
        for piece in [exchange(message, aside, 2 * step) for step in reversed(steps)]:
            incoming += piece.astype(F32)

    received = exchange(jnp.concatenate([incoming, near[0]], axis=1), 1, 1)
    return pl.pallas_call(
        last_kernel,
        out_shape=shaped(exciting.shape[1:], F32),
        in_specs=[SMEM] + [VMEM] * 5,
        out_specs=VMEM,
        compiler_params=PARAMS,
        name="last",
    )(core_at, incoming, near, received, down_maps[0], exciting_near)[None]


def solution(mesh):
    return jax.shard_map(
        functools.partial(local, mesh.shape["grp"], mesh.shape["body"]),
        mesh=mesh,
        in_specs=(
            P(("grp", "body"), None, None),
            P(("grp", "body"), None, None),
            P(("grp", "body"), None, None, None),
            P(),
            P(("grp", "body"), None),
            P("grp"),
            P(("grp", "body"), None, None, None),
            P(("grp", "body"), None, None, None),
            P("grp", None, None, "body", None),
        ),
        out_specs=P(("grp", "body"), None, None),
        check_vma=False,
    )
```

```python
import functools

import jax
import jax.numpy as jnp
from jax import lax
from jax.experimental import pallas as pl
from jax.experimental.pallas import tpu as pltpu
from jax.sharding import PartitionSpec as P

AXES = ("grp", "body")
SMEM = pl.BlockSpec(memory_space=pltpu.SMEM)
VMEM = pl.BlockSpec(memory_space=pltpu.VMEM)
HBM = pl.BlockSpec(memory_space=pltpu.HBM)
PARAMS = pltpu.CompilerParams(vmem_limit_bytes=8 << 20)
BF16, F32 = jnp.bfloat16, jnp.float32


def crossed(values):
    rows = values.shape[0] // 2
    real, imag = values[:rows], values[rows:]
    return jnp.concatenate(
        [jnp.concatenate([real, -imag], axis=1), jnp.concatenate([imag, real], axis=1)], axis=0
    )


def dot(left, right):
    return jnp.dot(left, right, preferred_element_type=F32)


def shaped(shape, dtype):
    return jax.ShapeDtypeStruct(shape, dtype)


def in_hbm(*arrays):
    return [pltpu.with_memory_space_constraint(array, pltpu.HBM) for array in arrays]


def first_kernel(
    incident_hbm, offsets_hbm, t_hbm, up_hbm, exciting_hbm,
    scattered, message, exciting, incident, offsets, t_mats, up, sems,
):
    sources = (incident_hbm, t_hbm, offsets_hbm, up_hbm, exciting_hbm)
    targets = (incident, t_mats, offsets, up, exciting)
    copies = [
        pltpu.make_async_copy(source, target, sems.at[i])
        for i, (source, target) in enumerate(zip(sources, targets))
    ]
    for copy in copies:
        copy.start()
    modes, coefs = up.shape[1:]
    rows = 2 * incident.shape[0]
    copies[0].wait()
    values = jnp.concatenate([incident[:, :modes], incident[:, modes:]], axis=0)
    values = crossed(values)
    copies[1].wait()
    own = dot(values, t_mats[...].reshape(2 * modes, modes)).astype(BF16)
    scattered[...] = own
    message[:rows, coefs:] = own.astype(F32)
    copies[2].wait()
    message[rows:, :] = jnp.zeros((message.shape[0] - rows, coefs + modes), F32)
    message[rows : rows + 1, : offsets.shape[1]] = offsets[...].astype(F32)
    own = crossed(own)
    copies[3].wait()
    message[:rows, :coefs] = dot(own, up[...].reshape(2 * modes, coefs))
    copies[4].wait()


def first_call(incident, offsets, t_mats, up, exciting):
    rows, modes, coefs = 2 * incident.shape[0], up.shape[1], up.shape[2]
    return pl.pallas_call(
        first_kernel,
        out_shape=(
            shaped((rows, modes), BF16),
            shaped((rows + 8, coefs + modes), F32),
            shaped(exciting.shape, F32),
        ),
        in_specs=[HBM] * 5,
        out_specs=(VMEM,) * 3,
        scratch_shapes=[
            pltpu.VMEM(incident.shape, BF16),
            pltpu.VMEM(offsets.shape, jnp.int32),
            pltpu.VMEM(t_mats.shape, BF16),
            pltpu.VMEM(up.shape, BF16),
            pltpu.SemaphoreType.DMA((5,)),
        ],
        compiler_params=PARAMS,
        name="first",
    )(*in_hbm(incident, offsets, t_mats, up, exciting))


def near_kernel(places, members, column, core, chip, indices, table, *rest):
    pieces, near = rest[:-1], rest[-1]
    rows, modes = near.shape
    half = modes // 2

    @pl.when(core[0] == 1)
    def _():
        total = jnp.zeros((rows, 2 * modes), F32)
        for other, piece, lane in places:
            for member in range(2):
                if other == 0 and member == column:
                    continue
                source = (chip[0] ^ other) * 2 + member
                slot = indices[2 * members + source]
                sequence = table[indices[column * members + slot]].astype(F32)
                mats = []
                for part in range(2):
                    band = jnp.broadcast_to(sequence[part : part + 1], (half, 2 * modes))
                    band = pltpu.roll(band, 0, 1, stride=1, stride_axis=0)
                    band = band.astype(BF16)
                    mats.append(
                        jnp.concatenate([band[:, modes:], band[:, half : half + modes]], axis=0)
                    )
                start = lane + member * modes
                values = pieces[piece][:, start : start + modes]
                total += dot(values, jnp.concatenate(mats, axis=1))
        top, low = total[: rows // 2], total[rows // 2 :]
        near[: rows // 2, :] = top[:, :modes] - low[:, modes:]
        near[rows // 2 :, :] = top[:, modes:] + low[:, :modes]


def group_kernel(places, core, group, own_maps, other_maps, *rest):
    pieces, incoming = rest[:-1], rest[-1]

    @pl.when(core[0] == 1)
    def _():
        total = jnp.zeros(incoming.shape, F32)
        for other, piece, index in places:
            source = group[0] ^ other
            mats = [
                maps[source, part] for part in range(2) for maps in (other_maps, own_maps)
            ]
            total += dot(crossed(pieces[piece][index]), jnp.concatenate(mats, axis=0))
        incoming[...] = total


def last_kernel(core, incoming, near, received, down, exciting, updated):
    coefs, modes = down.shape[1:]
    rows = exciting.shape[0]

    def finish(values, close):
        far = dot(crossed(values.astype(BF16)), down[...].reshape(2 * coefs, modes)) + close
        updated[:, :modes] = exciting[:, :modes] + far[:rows]
        updated[:, modes:] = exciting[:, modes:] + far[rows:]

    @pl.when(core[0] == 0)
    def _():
        finish(received[:, :coefs], received[:, coefs:])

    @pl.when(core[0] == 1)
    def _():
        finish(incoming[...], near[...])


def digits(count):
    bits = count.bit_length() - 1
    found = []
    while bits > 0:
        shift = bits - 2 if bits >= 2 else 0
        found.append([k << shift for k in range((1 << (bits - shift)) - 1, 0, -1)])
        bits = shift
    return found


def local(
    groups,
    bodies,
    incident,
    exciting,
    t_matrices,
    hankel_rows,
    offsets,
    lattice_slots,
    up_maps,
    down_maps,
    group_maps,
):
    body = lax.axis_index("body")
    group = lax.axis_index("grp")
    core, chip = body & 1, body >> 1
    chips = bodies // 2
    modes, coefs = up_maps.shape[2:]

    def exchange(values, even, odd):
        pairs = [(i, i ^ (odd if i % 2 else even)) for i in range(groups * bodies)]
        return lax.ppermute(values, AXES, pairs)

    core_at, chip_at, group_at = (x.astype(jnp.int32).reshape(1) for x in (core, chip, group))
    scattered, message, exciting_early = first_call(
        incident[0], offsets, t_matrices[0], up_maps[0], exciting[0]
    )
    rows = scattered.shape[0]
    received = exchange(message, 1, 1)
    other_maps = exchange(group_maps[0], 1, 1)

    expansion = message[:rows, :coefs] + received[:rows, :coefs]
    members = offsets.shape[1]
    indices = jnp.concatenate(
        [received[rows, :members].astype(jnp.int32), offsets[0], lattice_slots], axis=0
    )
    pieces = [jnp.concatenate([received[:rows, coefs:].astype(BF16), scattered], axis=1)]
    places = [(0, 0, 0)]
    aside = [bodies << bit for bit in range(groups.bit_length() - 1)] or [2]
    for steps in digits(chips):
        width = expansion.shape[1] // (len(steps) + 1)
        unit = min(steps)
        own = (chip // unit) % (len(steps) + 1)

        def part(index):
            return lax.dynamic_slice_in_dim(expansion, index * width, width, 1)

        gathered = [pieces[p][:, lane : lane + 2 * modes] for _, p, lane in places]
        messages = [
            jnp.concatenate(gathered + [part(own ^ (step // unit)).astype(BF16)], axis=1)
            for step in steps
        ]
        arrived = [
            exchange(message, aside[i % len(aside)], 2 * step)
            for i, (message, step) in enumerate(zip(messages, steps))
        ]
        held = len(places)
        expansion = part(own)
        for step, piece in zip(steps, arrived):
            expansion += piece[:, 2 * modes * held :].astype(F32)
            places += [
                (other ^ step, len(pieces), 2 * modes * i)
                for i, (other, _, _) in enumerate(places[:held])
            ]
            pieces.append(piece)

    def near_call(column, *pieces):
        size = len(pieces) * rows * modes * modes
        return pl.pallas_call(
            functools.partial(near_kernel, tuple(places), members, column),
            out_shape=shaped((rows, modes), F32),
            in_specs=[SMEM] * 3 + [VMEM] * (1 + len(pieces)),
            out_specs=VMEM,
            compiler_params=PARAMS,
            cost_estimate=pl.CostEstimate(flops=8 * size, bytes_accessed=size, transcendentals=0),
            name="near",
        )(core_at, chip_at, indices, hankel_rows, *pieces)

    near = [near_call(column, *pieces) for column in range(2)]

    blocks = [expansion.astype(BF16)[None]]
    group_places = [(0, 0, 0)]
    for steps in digits(groups):
        message = [blocks[b][i] for _, b, i in group_places]
        message = blocks[0] if len(message) == 1 else jnp.stack(message)
        held = list(group_places)
        for step in reversed(steps):
            group_places += [(other ^ step, len(blocks), i) for i, (other, _, _) in enumerate(held)]
            blocks.append(exchange(message, 2, step * bodies))
    incoming = pl.pallas_call(
        functools.partial(group_kernel, tuple(group_places[1:])),
        out_shape=shaped((rows, coefs), F32),
        in_specs=[SMEM] * 2 + [VMEM] * (2 + len(blocks)),
        out_specs=VMEM,
        compiler_params=PARAMS,
        name="group",
    )(core_at, group_at, group_maps[0], other_maps, *blocks)

    for steps in digits(chips):
        message = incoming.astype(BF16)
        arrived = [
            exchange(message, aside[i % len(aside)], 2 * step)
            for i, step in enumerate(reversed(steps))
        ]
        for piece in arrived:
            incoming += piece.astype(F32)

    received = exchange(jnp.concatenate([incoming, near[0]], axis=1), 1, 1)
    return pl.pallas_call(
        last_kernel,
        out_shape=shaped(exciting.shape[1:], F32),
        in_specs=[SMEM] + [VMEM] * 5,
        out_specs=VMEM,
        compiler_params=PARAMS,
        name="last",
    )(core_at, incoming, near[1], received, down_maps[0], exciting_early)[None]


def solution(mesh):
    return jax.shard_map(
        functools.partial(local, mesh.shape["grp"], mesh.shape["body"]),
        mesh=mesh,
        in_specs=(
            P(("grp", "body"), None, None),
            P(("grp", "body"), None, None),
            P(("grp", "body"), None, None, None),
            P(),
            P(("grp", "body"), None),
            P("grp"),
            P(("grp", "body"), None, None, None),
            P(("grp", "body"), None, None, None),
            P("grp", None, None, "body", None),
        ),
        out_specs=P(("grp", "body"), None, None),
        check_vma=False,
    )
```
